128 devices in a mesh: req: 2 (over core), ctx: 64 (over y, z, x).
Axes of the slice: x: 4, y: 4, z: 4, core: 2. Of those that a mesh axis runs over, the one named last changes fastest.
Arguments:
- queries: bfloat16 [128, 8192], P(('req', 'ctx')), parts along dimension 0, may hold values from -256 to 256
- new_kv: bfloat16 [128, 2, 1024], P(('req', 'ctx')), parts along dimension 0, may hold values from -12 to 12
- prefix_kv: bfloat16 [8, 65536, 2, 1024], P('req', 'ctx'), parts along dimension 0, may hold values from -4.5 to 4.5
- pool: bfloat16 [1024, 16, 2, 1024], P(('req', 'ctx')), parts along dimension 0, may hold values from -12 to 12
- out_weight: bfloat16 [8192, 8192], P('ctx'), may hold values from -0.0625 to 0.0625
- parents: int32 [128], P('req'), parts along dimension 0, may hold values from 0 to 63, as said below
- tail_table: int32 [128, 4], P('req'), parts along dimension 0, may hold values from 0 to 511, as said below
- fresh_slots: int32 [128], P('req'), parts along dimension 0, may hold values from 0 to 511, as said below
- tail_lengths: int32 [128], P('req'), parts along dimension 0, may hold values from 1 to 63
Outputs:
- attn_out: float32 [128, 8192], P(('req', 'ctx')), parts along dimension 0
- new_pool: bfloat16 [1024, 16, 2, 1024], P(('req', 'ctx')), parts along dimension 0
The draws below stay inside these ranges and needn't reach their ends.
There are 2 independent parts, one for each index of `req`. The reference program is written for one: setup_inputs(seed, part) draws one part's arguments, and reference() takes and returns one part's arrays. A program takes and returns all parts, laid end to end along the dimension named above; an argument that names none is the same for every part. Nothing has to cross between parts.
Inputs may be any that keep to these rules, and one draw needn't show every extreme that they name: `parents`: row i's parent is a beam of the same request, from 16 * (i // 16) to that plus 16 - 1. `tail_table`: all entries are distinct pool blocks, none among the last 2 blocks of a device's 8. Distinct pool blocks; fresh_slots[i] is one of the last 2 blocks of the device that holds beam row i, that is of device i.
All inputs are finite; a program needn't handle non-finite values.
Results may differ from the reference program's by a relative error of at most 0.0055.
Values may be sent and summed in bfloat16 or wider, within the bound.
A program may use at most 384 MiB of HBM per device.

```python
import jax
import jax.numpy as jnp
from jax import lax

D = 8192
HQ = 64
KVH = 8
HD = 128
BEAMS = 16
BLOCK = 16
TB = 4
CAP = 2
POOL_DEV = 8
ROW_DEV = 1
ROWS = 64
REQS = 4
PREFIX = 65536
NBLK = 512
QW = 8192
KVW = 1024


def attention_inputs(key):
    seeded = jax.random.fold_in(key, 7)
    subkeys = jax.random.split(seeded, 2)
    queries = jax.random.truncated_normal(subkeys[0], -4.5, 4.5, (ROWS, QW), jnp.float32)
    prefix = jax.random.truncated_normal(subkeys[1], -4.5, 4.5, (REQS, PREFIX, 2, KVW), jnp.float32)
    return (queries, prefix)


def draw_queries(key, part):
    return attention_inputs(key)[0].astype(jnp.bfloat16)


def draw_prefix_kv(key, part):
    return attention_inputs(key)[1].astype(jnp.bfloat16)


def draw_parents(key, part):
    seeded = jax.random.fold_in(key, 3)
    former_key, latter_key = jax.random.split(seeded)
    first_pick = jax.random.randint(former_key, (ROWS,), 0, BEAMS)
    second_pick = jax.random.randint(latter_key, (ROWS,), 0, BEAMS)
    row_ids = jnp.arange(ROWS, dtype=jnp.int32)
    request_base = row_ids // BEAMS * BEAMS
    within = row_ids % BEAMS
    picked = jnp.minimum(first_pick, second_pick)
    picked = jnp.where(within == 0, BEAMS - 1, jnp.where(within == 1, 0, picked))
    return (request_base + picked).astype(jnp.int32)


def slot_plan(key):
    seeded = jax.random.fold_in(key, 11)
    subkeys = jax.random.split(seeded, 2)
    device_count = NBLK // POOL_DEV
    old_per = POOL_DEV - CAP
    ordering = jax.random.permutation(subkeys[0], device_count * old_per)[:ROWS * TB]
    old_slots = ordering // old_per * POOL_DEV + ordering % old_per
    table = old_slots.reshape(ROWS, TB)
    row_ids = jnp.arange(ROWS, dtype=jnp.int32)
    home = row_ids // ROW_DEV
    rotation = jax.random.randint(subkeys[1], (device_count,), 0, CAP)
    place = (rotation[home] + row_ids % ROW_DEV) % CAP
    fresh = home * POOL_DEV + old_per + place
    return (table.astype(jnp.int32), fresh.astype(jnp.int32))


def draw_tail_table(key, part):
    return slot_plan(key)[0]


def draw_fresh_slots(key, part):
    return slot_plan(key)[1]


def with_ends(drawn, key, low, largest):
    spot = [jax.random.randint(jax.random.fold_in(key, axis), (), 0, length) for axis, length in enumerate(drawn.shape)]
    widest = drawn.shape.index(max(drawn.shape))
    neighbour = spot[:widest] + [(spot[widest] + 1) % drawn.shape[widest]] + spot[widest + 1:]
    return drawn.at[tuple(spot)].set(low).at[tuple(neighbour)].set(largest)


def steps_of(rng, dims, pieces, smallest, largest):
    gain = 1.0
    for axis_at, shards_of in pieces:
        steps = jax.random.uniform(jax.random.fold_in(jax.random.fold_in(rng, 6), axis_at), (shards_of,), jnp.float32, smallest / len(pieces), largest / len(pieces))
        gain = gain * jnp.repeat(jnp.exp(steps), dims[axis_at] // shards_of).reshape((-1,) + (1,) * (len(dims) - 1 - axis_at))
    return gain


def normal_values(stream_key, shape, width, most, shards=(), held_as=jnp.bfloat16):
    result = jax.random.normal(stream_key, shape, jnp.float32) * width
    if len(shards) > 0:
        result = steps_of(stream_key, shape, shards, -0.22, 0.18) * result
    return jnp.clip(result, min=-most, max=most).astype(held_as)


def setup_inputs(seed: int = 0, part: int = 0) -> dict:
    key_list = jax.random.split(jax.random.key(seed), 10)
    own_keys = jax.random.split(jax.random.fold_in(key_list[9], part), 10)
    return {
        "queries": draw_queries(jax.random.fold_in(jax.random.fold_in(key_list[9], part), 71), part),
        "new_kv": normal_values(own_keys[1], (ROWS, 2, KVW), 3.0, 12.0, ((0, 64),)),
        "prefix_kv": draw_prefix_kv(jax.random.fold_in(jax.random.fold_in(key_list[9], part), 71), part),
        "pool": normal_values(own_keys[3], (NBLK, BLOCK, 2, KVW), 3.0, 12.0, ((0, 64),)),
        "out_weight": normal_values(key_list[4], (QW, D), QW ** -0.5, 0.0625, ((0, 64),)),
        "parents": draw_parents(jax.random.fold_in(jax.random.fold_in(key_list[9], part), 71), part),
        "tail_table": draw_tail_table(jax.random.fold_in(jax.random.fold_in(key_list[9], part), 71), part),
        "fresh_slots": draw_fresh_slots(jax.random.fold_in(jax.random.fold_in(key_list[9], part), 71), part),
        "tail_lengths": with_ends(jax.random.randint(own_keys[8], (ROWS,), 1, TB * BLOCK), jax.random.fold_in(own_keys[8], 1), 1, (TB * BLOCK) - 1).astype(jnp.int32),
    }


masked_score = -1.0e30


def narrow(values):
    return lax.optimization_barrier(values.astype(jnp.bfloat16)).astype(jnp.float32)


def reference(queries, new_kv, prefix_kv, pool, out_weight, parents, tail_table, fresh_slots, tail_lengths):
    groups = HQ // KVH
    scaling = HD ** -0.5
    tail_len = TB * BLOCK
    highest_mode = lax.Precision.HIGHEST
    parent_len = tail_lengths[parents]
    parent_table = tail_table[parents]
    tail_blocks = pool[parent_table.reshape(-1)].reshape(ROWS, tail_len, 2, KVW)
    position = jnp.arange(tail_len, dtype=jnp.int32)
    live_mask = position[None, :] < parent_len[:, None]
    query_grid = queries.astype(jnp.float32).reshape(ROWS, KVH, groups, HD)
    tail_keys = tail_blocks[:, :, 0].astype(jnp.float32).reshape(ROWS, tail_len, KVH, HD)
    tail_vals = tail_blocks[:, :, 1].astype(jnp.float32).reshape(ROWS, tail_len, KVH, HD)
    tail_score = jnp.einsum("ikgd,itkd->ikgt", query_grid, tail_keys, precision=highest_mode) * scaling
    tail_score = jnp.where(live_mask[:, None, None, :], tail_score, masked_score)
    new_keys = new_kv[:, 0].astype(jnp.float32).reshape(ROWS, KVH, HD)
    new_vals = new_kv[:, 1].astype(jnp.float32).reshape(ROWS, KVH, HD)
    new_score = jnp.einsum("ikgd,ikd->ikg", query_grid, new_keys, precision=highest_mode) * scaling

    def one_request(inputs):
        req_query, req_prefix, req_tail_score, req_tail_vals, req_new_score, req_new_vals = inputs
        pre_keys = req_prefix[:, 0].astype(jnp.float32).reshape(PREFIX, KVH, HD)
        pre_vals = req_prefix[:, 1].astype(jnp.float32).reshape(PREFIX, KVH, HD)
        pre_score = jnp.einsum("bkgd,pkd->bkgp", req_query, pre_keys, precision=highest_mode) * scaling
        highest = jnp.maximum(jnp.maximum(pre_score.max(-1), req_tail_score.max(-1)), req_new_score)
        pre_exp = jnp.exp(pre_score - highest[..., None])
        tail_exp = jnp.exp(req_tail_score - highest[..., None])
        new_exp = jnp.exp(req_new_score - highest)
        totals = pre_exp.sum(-1) + tail_exp.sum(-1) + new_exp
        output = jnp.einsum("bkgp,pkd->bkgd", narrow(pre_exp), pre_vals, precision=highest_mode)
        output = output + jnp.einsum("bkgt,btkd->bkgd", narrow(tail_exp), req_tail_vals, precision=highest_mode)
        output = output + narrow(new_exp)[..., None] * req_new_vals[:, :, None, :]
        return (output / totals[..., None]).astype(jnp.bfloat16).reshape(BEAMS, QW)

    attended = lax.map(one_request, (
        query_grid.reshape(REQS, BEAMS, KVH, groups, HD),
        prefix_kv,
        tail_score.reshape(REQS, BEAMS, KVH, groups, tail_len),
        tail_vals.reshape(REQS, BEAMS, tail_len, KVH, HD),
        new_score.reshape(REQS, BEAMS, KVH, groups),
        new_vals.reshape(REQS, BEAMS, KVH, HD)))
    attended = attended.reshape(ROWS, QW)
    attn_out = jnp.dot(attended, out_weight, preferred_element_type=jnp.float32)
    offset = parent_len % BLOCK
    source = jnp.take_along_axis(parent_table, (parent_len // BLOCK)[:, None], axis=1)[:, 0]
    slot_pos = jnp.arange(BLOCK, dtype=jnp.int32)
    keep_old = (slot_pos[None, :] < offset[:, None])[:, :, None, None]
    copied = jnp.where(keep_old, pool[source], jnp.zeros((), jnp.bfloat16))
    write_new = (slot_pos[None, :] == offset[:, None])[:, :, None, None]
    copied = jnp.where(write_new, new_kv[:, None], copied)
    new_pool = pool.at[fresh_slots].set(copied)
    return attn_out, new_pool
```

```python
import functools
import math

import jax
import jax.numpy as jnp
from jax import lax
from jax.experimental import pallas as pl
from jax.experimental.pallas import tpu as pltpu
from jax.sharding import PartitionSpec as P

KVH = 8
HD = 128
GROUPS = 8
HQ = 64
N = 64
REQS = 4
BEAMS = 16
PRE = 1024
CHUNK = 128
PER_REQ = PRE // CHUNK
CHUNKS = REQS * PER_REQ
SLOTS = 4
TOKROWS = 16
BLK = 8
OLD = 6
NEG = -1e30
SCALE = HD ** (-0.5) * math.log2(math.e)
MESH = pl.DeviceIdType.MESH
F32 = jnp.float32
BF16 = jnp.bfloat16
PARTS = ((0, 3, "xzy"), (3, 6, "zyx"), (6, 8, "yxz"))


def dot_nt(a, b):
    return lax.dot_general(a, b, (((1,), (1,)), ((), ())), preferred_element_type=F32)


def dot_nn(a, b):
    return jnp.dot(a, b, preferred_element_type=F32)


def kernel(
    parents, table, fresh, lens, q_ref, newkv_ref, kv_hbm, pool_hbm, w_hbm,
    out_ref, newpool_ref,
    raw, stg, kd, kt, poolv, qstg, qbuf, qd, bias, osend, orecv, stat, srecv,
    wv, ystg, ysend, yrecv, relay, p2send, p2recv, blk,
    kv_sem, misc_sem, out_sem, q_ssem, q_rsem, o_ssem, o_rsem, s_ssem, s_rsem,
    y_ssem, y_rsem, p_ssem, p_rsem,
):
    core = lax.axis_index("req")
    me = lax.axis_index("ctx")
    y, z, x = me // 16, me // 4 % 4, me % 4

    def at(dy, dz, dx):
        return ((y + dy) % 4 * 4 + (z + dz) % 4) * 4 + (x + dx) % 4

    def peer(k):
        return at(k // 16, k // 4 % 4, k % 4)

    def remote(src, dst, ssem, rsem, dev):
        return pltpu.make_async_remote_copy(
            src_ref=src, dst_ref=dst, send_sem=ssem, recv_sem=rsem,
            device_id=(core, dev), device_id_type=MESH,
        )

    def await_bytes(ref, sem):
        pltpu.make_async_copy(ref, ref, sem).wait()

    def kv_copy(c):
        return pltpu.make_async_copy(
            kv_hbm.at[c // PER_REQ, pl.ds(c % PER_REQ * (CHUNK * TOKROWS), CHUNK * TOKROWS)],
            raw.at[c % SLOTS], kv_sem.at[c % SLOTS],
        )

    pool_copy = pltpu.make_async_copy(pool_hbm, poolv, misc_sem.at[0])
    w_copy = pltpu.make_async_copy(w_hbm, wv, misc_sem.at[1])
    pool_copy.start()
    for c in range(SLOTS):
        kv_copy(c).start()

    barrier = pltpu.get_barrier_semaphore()

    def greet(k, _):
        pl.semaphore_signal(barrier, inc=1, device_id=(core, peer(k)), device_id_type=MESH)
        return 0

    lax.fori_loop(1, N, greet, 0)

    for h in range(HQ):
        qstg[h : h + 1, :] = q_ref[:, h * HD : (h + 1) * HD].astype(F32)
    qbuf[y, z, x] = qstg[0:HQ, :].astype(BF16).reshape(KVH, GROUPS, HD)
    pl.semaphore_wait(barrier, N - 1)

    def q_copies(phase):
        made = []
        for p, (g0, g1, order) in enumerate(PARTS):
            axis = order[phase]
            seen = order[:phase]
            index = (
                slice(None) if "y" in seen else y,
                slice(None) if "z" in seen else z,
                slice(None) if "x" in seen else x,
                slice(g0, g1),
            )
            for d in range(1, 4):
                dev = at(d * (axis == "y"), d * (axis == "z"), d * (axis == "x"))
                made.append(remote(
                    qbuf.at[index], qbuf.at[index],
                    q_ssem.at[phase * 3 + p], q_rsem.at[phase * 3 + p], dev,
                ))
        return made

    def q_region(phase, p):
        g0, g1, _ = PARTS[p]
        rows = (
            (0, slice(0, 1), slice(0, 3)),
            (0, slice(0, 3), slice(None)),
            (slice(0, 3), slice(None), slice(None)),
        )[phase]
        return qbuf.at[rows + (slice(g0, g1),)]

    def q_send(phase):
        for copy in q_copies(phase):
            copy.start()

    def q_wait(phase):
        for p in range(3):
            await_bytes(q_region(phase, p), q_rsem.at[phase * 3 + p])

    q_send(0)

    pool_copy.wait()
    w_copy.start()

    def spread(dst, base):
        for j in range(TOKROWS):
            dst[j // 2, j % 2, pl.ds(base, CHUNK), :] = stg[
                pl.ds(j, CHUNK, stride=TOKROWS), :
            ].astype(BF16)

    stg[...] = poolv[...].reshape(CHUNK * TOKROWS, HD).astype(F32)
    stg[OLD * 16 * TOKROWS : (OLD * 16 + 1) * TOKROWS, :] = newkv_ref[...].astype(F32)
    spread(kt, 0)

    def piece(j):
        return poolv.at[pl.ds(j // 32 * 3, 3), j % 32]

    def to_relay(k, _):
        j = peer(k)
        remote(piece(j), relay.at[me], p_ssem.at[0], p_rsem.at[0], j).start()
        return 0

    lax.fori_loop(1, N, to_relay, 0)
    relay[me] = poolv[pl.ds(me // 32 * 3, 3), me % 32]

    lane = lax.broadcasted_iota(jnp.int32, (1, 128), 1)

    def mask_row(i, _):
        par = parents[i]
        length = lens[par]
        live = (lane == OLD * 16) & (jnp.full((1, 128), i, jnp.int32) == me)
        for j in range(4):
            block = table[j, par] - me * BLK
            live = live | ((lane // 16 == block) & (lane % 16 < length - 16 * j))
        bias[pl.ds(i, 1), :] = jnp.where(live, 0.0, NEG)
        return 0

    lax.fori_loop(0, N, mask_row, 0)

    def chunks(lo, hi):
        def body(c, _):
            kv_copy(c).wait()
            stg[...] = raw[c % SLOTS].astype(F32)

            @pl.when(c + SLOTS < CHUNKS)
            def _():
                kv_copy(c + SLOTS).start()

            spread(kd.at[c // PER_REQ], pl.multiple_of(c % PER_REQ * CHUNK, CHUNK))
            return 0

        lax.fori_loop(lo, hi, body, 0)

    chunks(0, 8)
    q_wait(0)
    q_send(1)
    chunks(8, 16)
    q_wait(1)
    q_send(2)
    chunks(16, 32)
    q_wait(2)

    await_bytes(relay.at[0:63], p_rsem.at[0])
    first = me // 32 * 3

    def pick(i, _):
        par = parents[i]
        source = table[lens[par] // 16, par]
        held = jnp.clip(source % BLK - first, 0, 2)
        p2send[i] = relay[source // BLK, held]
        return 0

    lax.fori_loop(0, N, pick, 0)

    def to_row(k, _):
        j = peer(k)
        remote(p2send.at[j], p2recv.at[me], p_ssem.at[1], p_rsem.at[1], j).start()
        return 0

    lax.fori_loop(1, N, to_row, 0)
    p2recv[me] = p2send[me]

    stat[...] = jnp.zeros_like(stat)
    sub16 = lax.broadcasted_iota(jnp.int32, (BEAMS, 128), 0)
    lane16 = lax.broadcasted_iota(jnp.int32, (BEAMS, 128), 1)

    def request(r, _):
        qstg[...] = qbuf[r].reshape(BEAMS * HQ, HD).astype(F32)
        for h in range(HQ):
            qd[h // GROUPS, h % GROUPS * BEAMS : (h % GROUPS + 1) * BEAMS, :] = qstg[
                pl.ds(h, BEAMS, stride=HQ), :
            ].astype(BF16)
        bias_r = bias[pl.ds(pl.multiple_of(r * BEAMS, BEAMS), BEAMS), :]
        bias_q = jnp.broadcast_to(bias_r[None], (GROUPS, BEAMS, 128)).reshape(128, 128)
        m_spot = lane16 == sub16 + r * BEAMS
        l_spot = lane16 == sub16 + r * BEAMS + 64

        def head(g, _):
            q = qd[g]
            s = dot_nt(q, kd[r, g, 0])
            st = dot_nt(q, kt[g, 0]) + bias_q
            top = jnp.maximum(s.max(-1, keepdims=True), st.max(-1, keepdims=True))
            e = jnp.exp2((s - top) * SCALE)
            et = jnp.exp2((st - top) * SCALE)
            total = e.sum(-1, keepdims=True) + et.sum(-1, keepdims=True)
            o = dot_nn(e.astype(BF16), kd[r, g, 1]) + dot_nn(et.astype(BF16), kt[g, 1])
            osend[r, pl.ds(g * GROUPS, GROUPS)] = o.astype(BF16).reshape(GROUPS, BEAMS, HD)
            top3 = jnp.broadcast_to(top, (128, 128)).reshape(GROUPS, BEAMS, 128)
            total3 = jnp.broadcast_to(total, (128, 128)).reshape(GROUPS, BEAMS, 128)
            both = jnp.where(m_spot[None], top3, jnp.where(l_spot[None], total3, 0.0))
            rows = pl.ds(pl.multiple_of(g * GROUPS, GROUPS), GROUPS)
            stat[rows, :] = stat[rows, :] + both.sum(1)
            return 0

        lax.fori_loop(0, KVH, head, 0)

        def send(k, _):
            j = peer(k)
            remote(osend.at[r, j], orecv.at[me, r], o_ssem.at[r], o_rsem.at[r], j).start()
            return 0

        lax.fori_loop(1, N, send, 0)
        orecv[me, r] = osend[r, me]
        return 0

    lax.fori_loop(0, REQS, request, 0)

    def send_stat(k, _):
        j = peer(k)
        remote(stat.at[pl.ds(j, 1)], srecv.at[pl.ds(me, 1)], s_ssem, s_rsem, j).start()
        return 0

    lax.fori_loop(1, N, send_stat, 0)
    srecv[pl.ds(me, 1), :] = stat[pl.ds(me, 1), :]

    await_bytes(p2recv.at[0:63], p_rsem.at[1])
    par = parents[me]
    length = lens[par]
    source = table[length // 16, par]
    half = source % BLK // 3 * 32
    off = length % 16
    kept_all = p2recv[pl.ds(half, 32)].astype(F32)
    stg[0 : 32 * 8, :] = kept_all.reshape(32 * 8, HD)
    slot = fresh[me] % BLK
    newkv = newkv_ref[...].astype(F32)
    for t in range(16):
        rows = slice(t * TOKROWS, (t + 1) * TOKROWS)
        where_t = jnp.full((TOKROWS, HD), t, jnp.int32)
        token = jnp.where(where_t < off, stg[rows, :], jnp.where(where_t == off, newkv, 0.0))
        for b in range(2):
            here = jnp.full((TOKROWS, HD), OLD + b, jnp.int32) == slot
            old = poolv[OLD + b, 2 * t : 2 * t + 2].astype(F32).reshape(TOKROWS, HD)
            blk[b, 2 * t : 2 * t + 2] = jnp.where(here, token, old).astype(BF16).reshape(2, 8, HD)
    keep_copy = pltpu.make_async_copy(poolv.at[0:OLD], newpool_ref.at[0:OLD], out_sem.at[0])
    new_copy = pltpu.make_async_copy(blk, newpool_ref.at[OLD:BLK], out_sem.at[1])
    keep_copy.start()
    new_copy.start()

    await_bytes(srecv.at[0:63], s_rsem)
    turned = srecv[...].T
    valid = lax.broadcasted_iota(jnp.int32, (64, 128), 1) < N
    tops = jnp.where(valid, turned[0:64], -3e38)
    sums = jnp.where(valid, turned[64:128], 0.0)
    top = tops.max(-1, keepdims=True)
    share = jnp.exp2((tops - top) * SCALE)
    share = share / (share * sums).sum(-1, keepdims=True)
    for r in range(REQS):
        await_bytes(orecv.at[0:63, r], o_rsem.at[r])
    acc = jnp.zeros((64, HD), F32)
    for s in range(N):
        acc = acc + share[:, s : s + 1] * orecv[s].reshape(64, HD).astype(F32)
    attended = acc.astype(BF16)

    w_copy.wait()
    for c in range(16):
        part = dot_nn(attended, wv[:, c * 512 : (c + 1) * 512])
        for j in range(4):
            ystg[pl.ds(c * 4 + j, N, stride=64), :] = part[:, j * HD : (j + 1) * HD]

    def pack(i, _):
        ysend[i] = ystg[pl.ds(pl.multiple_of(i * 64, 64), 64), :].astype(BF16)
        return 0

    lax.fori_loop(0, N, pack, 0)

    def send_y(k, _):
        j = peer(k)
        remote(ysend.at[j], yrecv.at[me], y_ssem, y_rsem, j).start()
        return 0

    lax.fori_loop(1, N, send_y, 0)
    yrecv[me] = ysend[me]
    await_bytes(yrecv.at[0:63], y_rsem)

    def add(s, total):
        return total + yrecv[s].astype(F32)

    out_ref[...] = lax.fori_loop(0, N, add, jnp.zeros((64, HD), F32))

    for phase in range(3):
        for p in range(3):
            await_bytes(q_region(phase, p), q_ssem.at[phase * 3 + p])
    await_bytes(relay.at[0:63], p_ssem.at[0])
    await_bytes(p2send.at[0:63], p_ssem.at[1])
    for r in range(REQS):
        await_bytes(orecv.at[0:63, r], o_ssem.at[r])
    await_bytes(srecv.at[0:63], s_ssem)
    await_bytes(ysend.at[0:63], y_ssem)
    keep_copy.wait()
    new_copy.wait()


def local(
    queries, new_kv, prefix_kv, pool, out_weight, parents, tail_table, fresh_slots, tail_lengths
):
    def rows_of(a):
        lead = a.shape[:-2]
        a = a.reshape(lead + (2, KVH, HD))
        k = len(lead)
        return a.transpose(tuple(range(k)) + (k + 1, k, k + 2))

    kv = rows_of(prefix_kv).reshape(REQS, PRE * TOKROWS, HD)
    pool_rows = rows_of(pool).reshape(BLK, 32, 8, HD)
    new_rows = rows_of(new_kv).reshape(TOKROWS, HD)
    smem = pl.BlockSpec(memory_space=pltpu.SMEM)
    vmem = pl.BlockSpec(memory_space=pltpu.VMEM)
    hbm = pl.BlockSpec(memory_space=pl.ANY)
    dma = pltpu.SemaphoreType.DMA
    out, new_pool = pl.pallas_call(
        kernel,
        out_shape=(
            jax.ShapeDtypeStruct((64, HD), F32),
            jax.ShapeDtypeStruct((BLK, 32, 8, HD), BF16),
        ),
        in_specs=[smem] * 4 + [vmem, vmem, hbm, hbm, hbm],
        out_specs=(vmem, hbm),
        scratch_shapes=[
            pltpu.VMEM((SLOTS, CHUNK * TOKROWS, HD), BF16),
            pltpu.VMEM((CHUNK * TOKROWS, HD), F32),
            pltpu.VMEM((REQS, KVH, 2, PRE, HD), BF16),
            pltpu.VMEM((KVH, 2, CHUNK, HD), BF16),
            pltpu.VMEM((BLK, 32, 8, HD), BF16),
            pltpu.VMEM((BEAMS * HQ, HD), F32),
            pltpu.VMEM((4, 4, 4, KVH, GROUPS, HD), BF16),
            pltpu.VMEM((KVH, 128, HD), BF16),
            pltpu.VMEM((N, 128), F32),
            pltpu.VMEM((REQS, HQ, BEAMS, HD), BF16),
            pltpu.VMEM((N, REQS, BEAMS, HD), BF16),
            pltpu.VMEM((HQ, 128), F32),
            pltpu.VMEM((128, 128), F32),
            pltpu.VMEM((HD, 8192), BF16),
            pltpu.VMEM((N * 64, HD), F32),
            pltpu.VMEM((N, 64, HD), BF16),
            pltpu.VMEM((N, 64, HD), BF16),
            pltpu.VMEM((N, 3, 8, HD), BF16),
            pltpu.VMEM((N, 8, HD), BF16),
            pltpu.VMEM((N, 8, HD), BF16),
            pltpu.VMEM((2, 32, 8, HD), BF16),
            dma((SLOTS,)), dma((2,)), dma((2,)),
            dma((9,)), dma((9,)), dma((REQS,)), dma((REQS,)), dma, dma,
            dma, dma, dma((2,)), dma((2,)),
        ],
        compiler_params=pltpu.CompilerParams(
            collective_id=0, has_side_effects=True, vmem_limit_bytes=56 << 20
        ),
        name="beam_decode",
    )(
        parents, tail_table.T, fresh_slots, tail_lengths,
        queries, new_rows, kv, pool_rows, out_weight,
    )
    new_pool = new_pool.reshape(BLK, 16, KVH, 2, HD).transpose(0, 1, 3, 2, 4)
    return out.reshape(1, 8192), new_pool.reshape(BLK, 16, 2, KVH * HD)


def solution(mesh):
    in_specs = (
        P(("req", "ctx"), None),
        P(("req", "ctx"), None, None),
        P("req", "ctx", None, None),
        P(("req", "ctx"), None, None, None),
        P("ctx", None),
        P("req"),
        P("req", None),
        P("req"),
        P("req"),
    )
    out_specs = (P(("req", "ctx"), None), P(("req", "ctx"), None, None, None))
    return jax.shard_map(local, mesh=mesh, in_specs=in_specs, out_specs=out_specs, check_vma=False)
```

```python
import functools
import math

import jax
import jax.numpy as jnp
from jax import lax
from jax.experimental import pallas as pl
from jax.experimental.pallas import tpu as pltpu
from jax.sharding import PartitionSpec as P

KVH = 8
HD = 128
GROUPS = 8
HQ = 64
N = 64
REQS = 4
BEAMS = 16
PRE = 1024
CHUNK = 128
PER_REQ = PRE // CHUNK
CHUNKS = REQS * PER_REQ
TOKROWS = 16
BLK = 8
OLD = 6
NEG = -1e30
SCALE = HD ** (-0.5) * math.log2(math.e)
MESH = pl.DeviceIdType.MESH
F32 = jnp.float32
BF16 = jnp.bfloat16
PARTS = ((0, 3, "xzy"), (3, 6, "zyx"), (6, 8, "yxz"))


def dot_nt(a, b):
    return lax.dot_general(a, b, (((1,), (1,)), ((), ())), preferred_element_type=F32)


def dot_nn(a, b):
    return jnp.dot(a, b, preferred_element_type=F32)


def kernel(
    parents, table, fresh, lens, q_ref, newkv_ref, kv_hbm, pool_hbm, w_hbm,
    out_ref, newpool_ref,
    raw, stg, kd, kt, poolv, poolz, qstg, qbuf, qd, bias, osend, orecv, stat, srecv,
    wv, ystg, ysend, y1, y2send, y2, y3send, y3, rx, rz, ry, p2send, p2x, p2z, p2y, blk,
    kv_sem, misc_sem, out_sem, q_ssem, q_rsem, o_ssem, o_rsem, s_ssem, s_rsem,
    y_ssem, y_rsem, p_ssem, p_rsem,
):
    core = lax.axis_index("req")
    me = lax.axis_index("ctx")
    y, z, x = me // 16, me // 4 % 4, me % 4

    def at(dy, dz, dx):
        return ((y + dy) % 4 * 4 + (z + dz) % 4) * 4 + (x + dx) % 4

    def remote(src, dst, ssem, rsem, dev):
        return pltpu.make_async_remote_copy(
            src_ref=src, dst_ref=dst, send_sem=ssem, recv_sem=rsem,
            device_id=(core, dev), device_id_type=MESH,
        )

    def await_bytes(ref, sem):
        pltpu.make_async_copy(ref, ref, sem).wait()

    def kv_copy(c):
        return pltpu.make_async_copy(
            kv_hbm.at[c // PER_REQ, pl.ds(c % PER_REQ * (CHUNK * TOKROWS), CHUNK * TOKROWS)],
            raw.at[c], kv_sem.at[c],
        )

    barrier = pltpu.get_barrier_semaphore()
    for d in range(1, 4):
        for dev in (at(d, 0, 0), at(0, d, 0), at(0, 0, d)):
            pl.semaphore_signal(barrier, inc=1, device_id=(core, dev), device_id_type=MESH)

    pool_copies = [
        pltpu.make_async_copy(pool_hbm.at[0:3], poolv.at[0], misc_sem.at[0]),
        pltpu.make_async_copy(pool_hbm.at[3:6], poolv.at[1], misc_sem.at[1]),
        pltpu.make_async_copy(pool_hbm.at[6:8], poolz, misc_sem.at[2]),
    ]
    w_copy = pltpu.make_async_copy(w_hbm, wv, misc_sem.at[3])
    for copy in pool_copies:
        copy.start()
    for c in range(CHUNKS):
        kv_copy(c).start()
    w_copy.start()

    for h in range(HQ):
        qstg[h : h + 1, :] = q_ref[:, h * HD : (h + 1) * HD].astype(F32)
    qbuf[y, z, x] = qstg[0:HQ, :].astype(BF16).reshape(KVH, GROUPS, HD)

    def q_copies(phase):
        made = []
        for p, (g0, g1, order) in enumerate(PARTS):
            axis = order[phase]
            seen = order[:phase]
            index = (
                slice(None) if "y" in seen else y,
                slice(None) if "z" in seen else z,
                slice(None) if "x" in seen else x,
                slice(g0, g1),
            )
            for d in range(1, 4):
                dev = at(d * (axis == "y"), d * (axis == "z"), d * (axis == "x"))
                made.append(remote(
                    qbuf.at[index], qbuf.at[index],
                    q_ssem.at[phase * 3 + p], q_rsem.at[phase * 3 + p], dev,
                ))
        return made

    def q_region(phase, p):
        g0, g1, _ = PARTS[p]
        rows = (
            (0, slice(0, 1), slice(0, 3)),
            (0, slice(0, 3), slice(None)),
            (slice(0, 3), slice(None), slice(None)),
        )[phase]
        return qbuf.at[rows + (slice(g0, g1),)]

    def q_send(phase):
        for copy in q_copies(phase):
            copy.start()

    def q_wait(phase):
        for p in range(3):
            await_bytes(q_region(phase, p), q_rsem.at[phase * 3 + p])

    for copy in pool_copies:
        copy.wait()

    def spread(dst, base):
        for j in range(TOKROWS):
            dst[j // 2, j % 2, pl.ds(base, CHUNK), :] = stg[
                pl.ds(j, CHUNK, stride=TOKROWS), :
            ].astype(BF16)

    stg[0 : OLD * 256, :] = poolv[...].reshape(OLD * 256, HD).astype(F32)
    stg[OLD * 256 :, :] = poolz[...].reshape((BLK - OLD) * 256, HD).astype(F32)
    stg[OLD * 256 : OLD * 256 + TOKROWS, :] = newkv_ref[...].astype(F32)
    spread(kt, 0)

    def along(d):
        return (y + d) % 4, (z + d) % 4, (x + d) % 4

    def leg1(phase):
        for d in range(1, 4):
            y2_, z2_, x2_ = along(d)
            src, dst, dev = (
                (poolv.at[:, :, :, :, x2_], rx.at[x], at(0, 0, d)),
                (rx.at[:, :, :, :, z2_], rz.at[z], at(0, d, 0)),
                (rz.at[:, :, y2_ // 2, :, y2_ % 2], ry.at[y], at(d, 0, 0)),
            )[phase]
            remote(src, dst, p_ssem.at[phase], p_rsem.at[phase], dev).start()
        if phase == 0:
            rx[x] = poolv[:, :, :, :, x]
        elif phase == 1:
            rz[z] = rx[:, :, :, :, z]
        else:
            ry[y] = rz[:, :, y // 2, :, y % 2]

    def leg1_wait(phase):
        await_bytes((rx, rz, ry)[phase].at[0:3], p_rsem.at[phase])

    def leg2(phase):
        for d in range(1, 4):
            y2_, z2_, x2_ = along(d)
            src, dst, dev = (
                (p2send.at[:, :, x2_], p2x.at[x], at(0, 0, d)),
                (p2x.at[:, :, z2_], p2z.at[z], at(0, d, 0)),
                (p2z.at[:, :, y2_], p2y.at[y], at(d, 0, 0)),
            )[phase]
            remote(src, dst, p_ssem.at[3 + phase], p_rsem.at[3 + phase], dev).start()
        if phase == 0:
            p2x[x] = p2send[:, :, x]
        elif phase == 1:
            p2z[z] = p2x[:, :, z]
        else:
            p2y[y] = p2z[:, :, y]

    def leg2_wait(phase):
        await_bytes((p2x, p2z, p2y)[phase].at[0:3], p_rsem.at[3 + phase])

    pl.semaphore_wait(barrier, 9)
    q_send(0)
    leg1(0)

    lane = lax.broadcasted_iota(jnp.int32, (1, 128), 1)

    def mask_row(i, _):
        par = parents[i]
        length = lens[par]
        live = (lane == OLD * 16) & (jnp.full((1, 128), i, jnp.int32) == me)
        for j in range(4):
            block = table[j, par] - me * BLK
            live = live | ((lane // 16 == block) & (lane % 16 < length - 16 * j))
        bias[pl.ds(i, 1), :] = jnp.where(live, 0.0, NEG)
        return 0

    lax.fori_loop(0, N, mask_row, 0, unroll=8)

    def chunks(lo, hi):
        def body(c, _):
            kv_copy(c).wait()
            stg[...] = raw[c].astype(F32)
            spread(kd.at[c // PER_REQ], pl.multiple_of(c % PER_REQ * CHUNK, CHUNK))
            return 0

        lax.fori_loop(lo, hi, body, 0)

    q_wait(0)
    q_send(1)
    chunks(0, 8)
    q_wait(1)
    q_send(2)
    leg1_wait(0)
    leg1(1)
    chunks(8, 32)
    q_wait(2)
    leg1_wait(1)
    leg1(2)

    first = me // 32 * 3

    def pick(i, _):
        par = parents[i]
        source = table[lens[par] // 16, par]
        held = jnp.clip(source % BLK - first, 0, 2)
        home = source // BLK
        p2send[i // 16, i // 4 % 4, i % 4] = ry[home // 16, home // 4 % 4, home % 4, held]
        return 0

    stat[...] = jnp.zeros_like(stat)
    sub16 = lax.broadcasted_iota(jnp.int32, (BEAMS, 128), 0)
    lane16 = lax.broadcasted_iota(jnp.int32, (BEAMS, 128), 1)

    def turn(r, _):
        qstg[...] = qbuf[r].reshape(BEAMS * HQ, HD).astype(F32)
        for h in range(HQ):
            qd[r, h // GROUPS, h % GROUPS * BEAMS : (h % GROUPS + 1) * BEAMS, :] = qstg[
                pl.ds(h, BEAMS, stride=HQ), :
            ].astype(BF16)
        return 0

    lax.fori_loop(0, REQS, turn, 0)
    own_group = me // GROUPS

    def group_of(t):
        return (own_group + t) % KVH

    def attend(t):
        r = t // KVH
        g = group_of(t)
        bias_r = bias[pl.ds(pl.multiple_of(r * BEAMS, BEAMS), BEAMS), :]
        bias_q = jnp.broadcast_to(bias_r[None], (GROUPS, BEAMS, 128)).reshape(128, 128)
        m_spot = lane16 == sub16 + r * BEAMS
        l_spot = lane16 == sub16 + r * BEAMS + 64
        q = qd[r, g]
        s = dot_nt(q, kd[r, g, 0])
        st = dot_nt(q, kt[g, 0]) + bias_q
        top = jnp.maximum(s.max(-1, keepdims=True), st.max(-1, keepdims=True))
        e = jnp.exp2((s - top) * SCALE)
        et = jnp.exp2((st - top) * SCALE)
        total = e.sum(-1, keepdims=True) + et.sum(-1, keepdims=True)
        o = dot_nn(e.astype(BF16), kd[r, g, 1]) + dot_nn(et.astype(BF16), kt[g, 1])
        osend[r, pl.ds(g * GROUPS, GROUPS)] = o.astype(BF16).reshape(GROUPS, BEAMS, HD)
        top3 = jnp.broadcast_to(top, (128, 128)).reshape(GROUPS, BEAMS, 128)
        total3 = jnp.broadcast_to(total, (128, 128)).reshape(GROUPS, BEAMS, 128)
        both = jnp.where(m_spot[None], top3, jnp.where(l_spot[None], total3, 0.0))
        rows = pl.ds(pl.multiple_of(g * GROUPS, GROUPS), GROUPS)
        stat[rows, :] = stat[rows, :] + both.sum(1)

    def send(t, last):
        r = t // KVH
        g = group_of(t)
        for j in range(GROUPS):
            dev = g * GROUPS + (me + j) % GROUPS

            def start(dev=dev):
                remote(osend.at[r, dev], orecv.at[me, r], o_ssem.at[r], o_rsem.at[r], dev).start()
                if last:
                    remote(
                        stat.at[pl.ds(dev, 1)], srecv.at[pl.ds(me, 1)], s_ssem, s_rsem, dev
                    ).start()

            if j == 0:
                pl.when(t % KVH != 0)(start)
            else:
                start()

    def steps(lo, hi, last):
        def step(t, _):
            send(t - 1, last)
            attend(t)
            return 0

        lax.fori_loop(lo, hi, step, 0)

    attend(0)
    steps(1, 8, False)
    leg1_wait(2)
    lax.fori_loop(0, N, pick, 0, unroll=8)
    leg2(0)
    steps(8, 16, False)
    leg2_wait(0)
    leg2(1)
    steps(16, 25, False)
    leg2_wait(1)
    leg2(2)
    steps(25, 32, True)
    send(jnp.int32(31), True)
    for r in range(REQS):
        orecv[me, r] = osend[r, me]
    srecv[pl.ds(me, 1), :] = stat[pl.ds(me, 1), :]

    leg2_wait(2)
    par = parents[me]
    length = lens[par]
    source = table[length // 16, par]
    half = source % BLK // 3 * 2
    off = length % 16
    kept_all = p2y[pl.ds(half, 2)].astype(F32)
    stg[0 : 32 * 8, :] = kept_all.reshape(32 * 8, HD)
    slot = fresh[me] % BLK
    newkv = newkv_ref[...].astype(F32)
    for t in range(16):
        rows = slice(t * TOKROWS, (t + 1) * TOKROWS)
        where_t = jnp.full((TOKROWS, HD), t, jnp.int32)
        token = jnp.where(where_t < off, stg[rows, :], jnp.where(where_t == off, newkv, 0.0))
        for b in range(2):
            here = jnp.full((TOKROWS, HD), OLD + b, jnp.int32) == slot
            at_t = (b, t // 8, t // 2 % 4, slice(t % 2 * 2, t % 2 * 2 + 2))
            old = poolz[at_t].astype(F32).reshape(TOKROWS, HD)
            blk[at_t] = jnp.where(here, token, old).astype(BF16).reshape(2, 8, HD)
    keep_copies = [
        pltpu.make_async_copy(poolv.at[0], newpool_ref.at[0:3], out_sem.at[0]),
        pltpu.make_async_copy(poolv.at[1], newpool_ref.at[3:6], out_sem.at[1]),
        pltpu.make_async_copy(blk, newpool_ref.at[6:8], out_sem.at[2]),
    ]
    for copy in keep_copies:
        copy.start()

    await_bytes(srecv.at[0:63], s_rsem)
    turned = srecv[...].T
    valid = lax.broadcasted_iota(jnp.int32, (64, 128), 1) < N
    tops = jnp.where(valid, turned[0:64], -3e38)
    sums = jnp.where(valid, turned[64:128], 0.0)
    top = tops.max(-1, keepdims=True)
    share = jnp.exp2((tops - top) * SCALE)
    share = share / (share * sums).sum(-1, keepdims=True)
    for r in range(REQS):
        await_bytes(orecv.at[0:63, r], o_rsem.at[r])
    acc = jnp.zeros((64, HD), F32)
    for s in range(N):
        acc = acc + share[:, s : s + 1] * orecv[s].reshape(64, HD).astype(F32)
    attended = acc.astype(BF16)

    w_copy.wait()

    def y_pick(ref, order, phase, index, c0, c1):
        rows = []
        for name in "yzx":
            if name in order[:phase]:
                continue
            rows.append(index if name == order[phase] else slice(None))
        return ref.at[tuple(rows) + (slice(c0, c1),)]

    def y_copies(p, phase):
        c0, c1, order = PARTS[p]
        axis = order[phase]
        made = []
        for d in range(1, 4):
            mine = {"y": (y + d) % 4, "z": (z + d) % 4, "x": (x + d) % 4}[axis]
            src = y_pick((ysend, y2send, y3send)[phase], order, phase, mine, c0, c1)
            lead = (slice(None),) * (2 - phase)
            dst = (y1, y2, y3)[phase].at[(d - 1,) + lead + (slice(c0, c1),)]
            dev = at(d * (axis == "y"), d * (axis == "z"), d * (axis == "x"))
            made.append(remote(src, dst, y_ssem.at[phase * 3 + p], y_rsem.at[phase * 3 + p], dev))
        return made

    def y_region(p, phase):
        c0, c1, _ = PARTS[p]
        lead = (slice(None),) * (3 - phase)
        return (y1, y2, y3)[phase].at[lead + (slice(c0, c1),)]

    def y_total(p, phase):
        c0, c1, order = PARTS[p]
        await_bytes(y_region(p, phase), y_rsem.at[phase * 3 + p])
        mine = {"y": y, "z": z, "x": x}[order[phase]]
        total = y_pick((ysend, y2send, y3send)[phase], order, phase, mine, c0, c1)[...].astype(F32)
        lead = (slice(None),) * (2 - phase)
        for d in range(3):
            total = total + (y1, y2, y3)[phase][(d,) + lead + (slice(c0, c1),)].astype(F32)
        return total

    for p, (c0, c1, _) in enumerate(PARTS):
        for c in range(c0 * 2, c1 * 2):
            part = dot_nn(attended, wv[:, c * 512 : (c + 1) * 512])
            for j in range(4):
                ystg[pl.ds(c * 4 + j, N, stride=64), :] = part[:, j * HD : (j + 1) * HD]

        def pack(i, _, c0=c0, c1=c1):
            rows = ystg[pl.ds(pl.multiple_of(i * 64 + c0 * 8, 8), (c1 - c0) * 8), :]
            ysend[i // 16, i // 4 % 4, i % 4, c0:c1] = rows.astype(BF16).reshape(c1 - c0, 8, HD)
            return 0

        lax.fori_loop(0, N, pack, 0, unroll=4)
        for copy in y_copies(p, 0):
            copy.start()
    for p, (c0, c1, _) in enumerate(PARTS):
        y2send[:, :, c0:c1] = y_total(p, 0).astype(BF16)
        for copy in y_copies(p, 1):
            copy.start()
    for p, (c0, c1, _) in enumerate(PARTS):
        y3send[:, c0:c1] = y_total(p, 1)
        for copy in y_copies(p, 2):
            copy.start()
    for p, (c0, c1, _) in enumerate(PARTS):
        out_ref[c0 * 8 : c1 * 8, :] = y_total(p, 2).reshape((c1 - c0) * 8, HD)

    for phase in range(3):
        for p in range(3):
            await_bytes(q_region(phase, p), q_ssem.at[phase * 3 + p])
            await_bytes(y_region(p, phase), y_ssem.at[phase * 3 + p])
        await_bytes((rx, rz, ry)[phase].at[0:3], p_ssem.at[phase])
        await_bytes((p2x, p2z, p2y)[phase].at[0:3], p_ssem.at[3 + phase])
    for r in range(REQS):
        await_bytes(orecv.at[0:63, r], o_ssem.at[r])
    await_bytes(srecv.at[0:63], s_ssem)
    for copy in keep_copies:
        copy.wait()


def local(
    queries, new_kv, prefix_kv, pool, out_weight, parents, tail_table, fresh_slots, tail_lengths
):
    def rows_of(a):
        lead = a.shape[:-2]
        a = a.reshape(lead + (2, KVH, HD))
        k = len(lead)
        return a.transpose(tuple(range(k)) + (k + 1, k, k + 2))

    kv = rows_of(prefix_kv).reshape(REQS, PRE * TOKROWS, HD)
    pool_rows = rows_of(pool).reshape(BLK, 2, 4, 4, 8, HD)
    new_rows = rows_of(new_kv).reshape(TOKROWS, HD)
    smem = pl.BlockSpec(memory_space=pltpu.SMEM)
    vmem = pl.BlockSpec(memory_space=pltpu.VMEM)
    hbm = pl.BlockSpec(memory_space=pl.ANY)
    dma = pltpu.SemaphoreType.DMA
    out, new_pool = pl.pallas_call(
        kernel,
        out_shape=(
            jax.ShapeDtypeStruct((64, HD), F32),
            jax.ShapeDtypeStruct((BLK, 2, 4, 4, 8, HD), BF16),
        ),
        in_specs=[smem] * 4 + [vmem, vmem, hbm, hbm, hbm],
        out_specs=(vmem, hbm),
        scratch_shapes=[
            pltpu.VMEM((CHUNKS, CHUNK * TOKROWS, HD), BF16),
            pltpu.VMEM((CHUNK * TOKROWS, HD), F32),
            pltpu.VMEM((REQS, KVH, 2, PRE, HD), BF16),
            pltpu.VMEM((KVH, 2, CHUNK, HD), BF16),
            pltpu.VMEM((2, 3, 2, 4, 4, 8, HD), BF16),
            pltpu.VMEM((2, 2, 4, 4, 8, HD), BF16),
            pltpu.VMEM((BEAMS * HQ, HD), F32),
            pltpu.VMEM((4, 4, 4, KVH, GROUPS, HD), BF16),
            pltpu.VMEM((REQS, KVH, 128, HD), BF16),
            pltpu.VMEM((N, 128), F32),
            pltpu.VMEM((REQS, HQ, BEAMS, HD), BF16),
            pltpu.VMEM((N, REQS, BEAMS, HD), BF16),
            pltpu.VMEM((HQ, 128), F32),
            pltpu.VMEM((128, 128), F32),
            pltpu.VMEM((HD, 8192), BF16),
            pltpu.VMEM((N * 64, HD), F32),
            pltpu.VMEM((4, 4, 4, 8, 8, HD), BF16),
            pltpu.VMEM((3, 4, 4, 8, 8, HD), BF16),
            pltpu.VMEM((4, 4, 8, 8, HD), BF16),
            pltpu.VMEM((3, 4, 8, 8, HD), BF16),
            pltpu.VMEM((4, 8, 8, HD), F32),
            pltpu.VMEM((3, 8, 8, HD), F32),
            pltpu.VMEM((4, 2, 3, 2, 4, 8, HD), BF16),
            pltpu.VMEM((4, 4, 2, 3, 2, 8, HD), BF16),
            pltpu.VMEM((4, 4, 4, 3, 8, HD), BF16),
            pltpu.VMEM((4, 4, 4, 8, HD), BF16),
            pltpu.VMEM((4, 4, 4, 8, HD), BF16),
            pltpu.VMEM((4, 4, 4, 8, HD), BF16),
            pltpu.VMEM((4, 4, 4, 8, HD), BF16),
            pltpu.VMEM((2, 2, 4, 4, 8, HD), BF16),
            dma((CHUNKS,)), dma((4,)), dma((3,)),
            dma((9,)), dma((9,)), dma((REQS,)), dma((REQS,)), dma, dma,
            dma((9,)), dma((9,)), dma((6,)), dma((6,)),
        ],
        compiler_params=pltpu.CompilerParams(
            collective_id=0, has_side_effects=True, vmem_limit_bytes=56 << 20
        ),
        name="beam_decode",
    )(
        parents, tail_table.T, fresh_slots, tail_lengths,
        queries, new_rows, kv, pool_rows, out_weight,
    )
    new_pool = new_pool.reshape(BLK, 16, KVH, 2, HD).transpose(0, 1, 3, 2, 4)
    return out.reshape(1, 8192), new_pool.reshape(BLK, 16, 2, KVH * HD)


def solution(mesh):
    in_specs = (
        P(("req", "ctx"), None),
        P(("req", "ctx"), None, None),
        P("req", "ctx", None, None),
        P(("req", "ctx"), None, None, None),
        P("ctx", None),
        P("req"),
        P("req", None),
        P("req"),
        P("req"),
    )
    out_specs = (P(("req", "ctx"), None), P(("req", "ctx"), None, None, None))
    return jax.shard_map(local, mesh=mesh, in_specs=in_specs, out_specs=out_specs, check_vma=False)
```

```python
import functools
import math

import jax
import jax.numpy as jnp
from jax import lax
from jax.experimental import pallas as pl
from jax.experimental.pallas import tpu as pltpu
from jax.sharding import PartitionSpec as P

KVH = 8
HD = 128
GROUPS = 8
HQ = 64
N = 64
REQS = 4
BEAMS = 16
PRE = 1024
CHUNK = 128
PER_REQ = PRE // CHUNK
CHUNKS = REQS * PER_REQ
TOKROWS = 16
BLK = 8
OLD = 6
NEG = -1e30
SCALE = HD ** (-0.5) * math.log2(math.e)
MESH = pl.DeviceIdType.MESH
F32 = jnp.float32
BF16 = jnp.bfloat16
PARTS = ((0, 3, "xzy"), (3, 6, "zyx"), (6, 8, "yxz"))


def dot_nt(a, b):
    return lax.dot_general(a, b, (((1,), (1,)), ((), ())), preferred_element_type=F32)


def dot_nn(a, b):
    return jnp.dot(a, b, preferred_element_type=F32)


def kernel(
    parents, table, fresh, lens, q_ref, newkv_ref, kv_hbm, pool_hbm, w_hbm,
    out_ref, newpool_ref,
    raw, stg, kd, kt, poolv, poolz, qstg, qbuf, qd, bias, osend, orecv, stat, srecv,
    wv, ystg, ysend, yrecv, rx, rz, ry, p2send, p2x, p2z, p2y, blk,
    kv_sem, misc_sem, out_sem, q_ssem, q_rsem, o_ssem, o_rsem, s_ssem, s_rsem,
    y_ssem, y_rsem, p_ssem, p_rsem,
):
    core = lax.axis_index("req")
    me = lax.axis_index("ctx")
    y, z, x = me // 16, me // 4 % 4, me % 4

    def at(dy, dz, dx):
        return ((y + dy) % 4 * 4 + (z + dz) % 4) * 4 + (x + dx) % 4

    def peer(k):
        return at(k // 16, k // 4 % 4, k % 4)

    def remote(src, dst, ssem, rsem, dev):
        return pltpu.make_async_remote_copy(
            src_ref=src, dst_ref=dst, send_sem=ssem, recv_sem=rsem,
            device_id=(core, dev), device_id_type=MESH,
        )

    def await_bytes(ref, sem):
        pltpu.make_async_copy(ref, ref, sem).wait()

    def kv_copy(c):
        return pltpu.make_async_copy(
            kv_hbm.at[c // PER_REQ, pl.ds(c % PER_REQ * (CHUNK * TOKROWS), CHUNK * TOKROWS)],
            raw.at[c], kv_sem.at[c],
        )

    barrier = pltpu.get_barrier_semaphore()
    for d in range(1, 4):
        for dev in (at(d, 0, 0), at(0, d, 0), at(0, 0, d)):
            pl.semaphore_signal(barrier, inc=1, device_id=(core, dev), device_id_type=MESH)

    pool_copies = [
        pltpu.make_async_copy(pool_hbm.at[0:3], poolv.at[0], misc_sem.at[0]),
        pltpu.make_async_copy(pool_hbm.at[3:6], poolv.at[1], misc_sem.at[1]),
        pltpu.make_async_copy(pool_hbm.at[6:8], poolz, misc_sem.at[2]),
    ]
    w_copy = pltpu.make_async_copy(w_hbm, wv, misc_sem.at[3])
    for copy in pool_copies:
        copy.start()

    def start_kv(c, _):
        kv_copy(c).start()
        return 0

    lax.fori_loop(0, CHUNKS, start_kv, 0)
    w_copy.start()

    for h in range(HQ):
        qstg[h : h + 1, :] = q_ref[:, h * HD : (h + 1) * HD].astype(F32)
    qbuf[y, z, x] = qstg[0:HQ, :].astype(BF16).reshape(KVH, GROUPS, HD)

    def q_copies(phase):
        made = []
        for p, (g0, g1, order) in enumerate(PARTS):
            axis = order[phase]
            seen = order[:phase]
            index = (
                slice(None) if "y" in seen else y,
                slice(None) if "z" in seen else z,
                slice(None) if "x" in seen else x,
                slice(g0, g1),
            )
            for d in range(1, 4):
                dev = at(d * (axis == "y"), d * (axis == "z"), d * (axis == "x"))
                made.append(remote(
                    qbuf.at[index], qbuf.at[index],
                    q_ssem.at[phase * 3 + p], q_rsem.at[phase * 3 + p], dev,
                ))
        return made

    def q_region(phase, p):
        g0, g1, _ = PARTS[p]
        rows = (
            (0, slice(0, 1), slice(0, 3)),
            (0, slice(0, 3), slice(None)),
            (slice(0, 3), slice(None), slice(None)),
        )[phase]
        return qbuf.at[rows + (slice(g0, g1),)]

    def q_send(phase):
        for copy in q_copies(phase):
            copy.start()

    def q_wait(phase):
        for p in range(3):
            await_bytes(q_region(phase, p), q_rsem.at[phase * 3 + p])

    for copy in pool_copies:
        copy.wait()
    keep_copies = [
        pltpu.make_async_copy(poolv.at[0], newpool_ref.at[0:3], out_sem.at[0]),
        pltpu.make_async_copy(poolv.at[1], newpool_ref.at[3:6], out_sem.at[1]),
    ]
    for copy in keep_copies:
        copy.start()

    def spread(dst, base):
        for j in range(TOKROWS):
            dst[j // 2, j % 2, pl.ds(base, CHUNK), :] = stg[
                pl.ds(j, CHUNK, stride=TOKROWS), :
            ].astype(BF16)

    stg[0 : OLD * 256, :] = poolv[...].reshape(OLD * 256, HD).astype(F32)
    stg[OLD * 256 :, :] = poolz[...].reshape((BLK - OLD) * 256, HD).astype(F32)
    stg[OLD * 256 : OLD * 256 + TOKROWS, :] = newkv_ref[...].astype(F32)
    spread(kt, 0)

    def along(d):
        return (y + d) % 4, (z + d) % 4, (x + d) % 4

    def leg1(phase):
        for d in range(1, 4):
            y2_, z2_, x2_ = along(d)
            src, dst, dev = (
                (poolv.at[:, :, :, :, x2_], rx.at[x], at(0, 0, d)),
                (rx.at[:, :, :, :, z2_], rz.at[z], at(0, d, 0)),
                (rz.at[:, :, y2_ // 2, :, y2_ % 2], ry.at[y], at(d, 0, 0)),
            )[phase]
            remote(src, dst, p_ssem.at[phase], p_rsem.at[phase], dev).start()
        if phase == 0:
            rx[x] = poolv[:, :, :, :, x]
        elif phase == 1:
            rz[z] = rx[:, :, :, :, z]
        else:
            ry[y] = rz[:, :, y // 2, :, y % 2]

    def leg1_wait(phase):
        await_bytes((rx, rz, ry)[phase].at[0:3], p_rsem.at[phase])

    def leg2(phase):
        for d in range(1, 4):
            y2_, z2_, x2_ = along(d)
            src, dst, dev = (
                (p2send.at[:, :, x2_], p2x.at[x], at(0, 0, d)),
                (p2x.at[:, :, z2_], p2z.at[z], at(0, d, 0)),
                (p2z.at[:, :, y2_], p2y.at[y], at(d, 0, 0)),
            )[phase]
            remote(src, dst, p_ssem.at[3 + phase], p_rsem.at[3 + phase], dev).start()
        if phase == 0:
            p2x[x] = p2send[:, :, x]
        elif phase == 1:
            p2z[z] = p2x[:, :, z]
        else:
            p2y[y] = p2z[:, :, y]

    def leg2_wait(phase):
        await_bytes((p2x, p2z, p2y)[phase].at[0:3], p_rsem.at[3 + phase])

    pl.semaphore_wait(barrier, 9)
    q_send(0)
    leg1(0)

    lane = lax.broadcasted_iota(jnp.int32, (1, 128), 1)

    def mask_row(i, _):
        par = parents[i]
        length = lens[par]
        live = (lane == OLD * 16) & (jnp.full((1, 128), i, jnp.int32) == me)
        for j in range(4):
            block = table[j, par] - me * BLK
            live = live | ((lane // 16 == block) & (lane % 16 < length - 16 * j))
        bias[pl.ds(i, 1), :] = jnp.where(live, 0.0, NEG)
        return 0

    lax.fori_loop(0, N, mask_row, 0, unroll=2)

    def chunks(lo, hi):
        def body(c, _):
            kv_copy(c).wait()
            stg[...] = raw[c].astype(F32)
            spread(kd.at[c // PER_REQ], pl.multiple_of(c % PER_REQ * CHUNK, CHUNK))
            return 0

        lax.fori_loop(lo, hi, body, 0)

    q_wait(0)
    q_send(1)
    chunks(0, 8)
    q_wait(1)
    q_send(2)
    leg1_wait(0)
    leg1(1)
    chunks(8, 32)
    q_wait(2)
    leg1_wait(1)
    leg1(2)

    first = me // 32 * 3

    def pick(i, _):
        par = parents[i]
        source = table[lens[par] // 16, par]
        held = jnp.clip(source % BLK - first, 0, 2)
        home = source // BLK
        p2send[i // 16, i // 4 % 4, i % 4] = ry[home // 16, home // 4 % 4, home % 4, held]
        return 0

    stat[...] = jnp.zeros_like(stat)
    sub16 = lax.broadcasted_iota(jnp.int32, (BEAMS, 128), 0)
    lane16 = lax.broadcasted_iota(jnp.int32, (BEAMS, 128), 1)

    def turn(r, _):
        qstg[...] = qbuf[r].reshape(BEAMS * HQ, HD).astype(F32)
        for h in range(HQ):
            qd[r, h // GROUPS, h % GROUPS * BEAMS : (h % GROUPS + 1) * BEAMS, :] = qstg[
                pl.ds(h, BEAMS, stride=HQ), :
            ].astype(BF16)
        return 0

    lax.fori_loop(0, REQS, turn, 0)
    own_group = me // GROUPS

    def group_of(t):
        return (own_group + t) % KVH

    def attend(r, g):
        bias_r = bias[pl.ds(pl.multiple_of(r * BEAMS, BEAMS), BEAMS), :]
        bias_q = jnp.broadcast_to(bias_r[None], (GROUPS, BEAMS, 128)).reshape(128, 128)
        m_spot = lane16 == sub16 + r * BEAMS
        l_spot = lane16 == sub16 + r * BEAMS + 64
        q = qd[r, g]
        s = dot_nt(q, kd[r, g, 0])
        st = dot_nt(q, kt[g, 0]) + bias_q
        top = jnp.maximum(s.max(-1, keepdims=True), st.max(-1, keepdims=True))
        e = jnp.exp2((s - top) * SCALE)
        et = jnp.exp2((st - top) * SCALE)
        total = e.sum(-1, keepdims=True) + et.sum(-1, keepdims=True)
        o = dot_nn(e.astype(BF16), kd[r, g, 1]) + dot_nn(et.astype(BF16), kt[g, 1])
        osend[r, pl.ds(g * GROUPS, GROUPS)] = o.astype(BF16).reshape(GROUPS, BEAMS, HD)
        top3 = jnp.broadcast_to(top, (128, 128)).reshape(GROUPS, BEAMS, 128)
        total3 = jnp.broadcast_to(total, (128, 128)).reshape(GROUPS, BEAMS, 128)
        both = jnp.where(m_spot[None], top3, jnp.where(l_spot[None], total3, 0.0))
        rows = pl.ds(pl.multiple_of(g * GROUPS, GROUPS), GROUPS)
        stat[rows, :] = stat[rows, :] + both.sum(1)

    def send(half, g):
        pair = pl.ds(half * 2, 2)

        def to(j, _):
            dev = g * GROUPS + (me + j) % GROUPS
            remote(
                osend.at[pair, dev], orecv.at[me, pair], o_ssem.at[half], o_rsem.at[half], dev
            ).start()

            @pl.when(half == 1)
            def _():
                remote(stat.at[pl.ds(dev, 1)], srecv.at[pl.ds(me, 1)], s_ssem, s_rsem, dev).start()

            return 0

        lax.fori_loop(jnp.where(g == own_group, 1, 0), GROUPS, to, 0)

    def step(u, _):
        @pl.when(u == 6)
        def _():
            leg1_wait(2)
            lax.fori_loop(0, N, pick, 0, unroll=8)
            leg2(0)

        @pl.when(u == 11)
        def _():
            leg2_wait(0)
            leg2(1)

        half = u // KVH
        g = group_of(u)
        attend(half * 2, g)
        attend(half * 2 + 1, g)
        send(half, g)
        return 0

    lax.fori_loop(0, 2 * KVH, step, 0)
    leg2_wait(1)
    leg2(2)
    orecv[me] = osend[:, me]
    srecv[pl.ds(me, 1), :] = stat[pl.ds(me, 1), :]

    await_bytes(srecv.at[0:63], s_rsem)
    turned = srecv[...].T
    valid = lax.broadcasted_iota(jnp.int32, (64, 128), 1) < N
    tops = jnp.where(valid, turned[0:64], -3e38)
    sums = jnp.where(valid, turned[64:128], 0.0)
    top = tops.max(-1, keepdims=True)
    share = jnp.exp2((tops - top) * SCALE)
    share = share / (share * sums).sum(-1, keepdims=True)
    for half in range(2):
        await_bytes(orecv.at[0:63, half * 2 : half * 2 + 2], o_rsem.at[half])

    def merge(s, carry):
        acc, turning = carry
        for k in range(4):
            acc = acc + turning[:, k : k + 1] * orecv[s * 4 + k].reshape(64, HD).astype(F32)
        return acc, pltpu.roll(turning, 124, 1)

    acc, _ = lax.fori_loop(0, N // 4, merge, (jnp.zeros((64, HD), F32), share))
    attended = acc.astype(BF16)

    w_copy.wait()

    def project(c, _):
        part = dot_nn(attended, wv[:, pl.ds(pl.multiple_of(c * 512, 512), 512)])
        for j in range(4):
            ystg[pl.ds(c * 4 + j, N, stride=72), :] = part[:, j * HD : (j + 1) * HD]
        return 0

    lax.fori_loop(0, 16, project, 0)

    def pack(i):
        ysend[i] = ystg[pl.ds(pl.multiple_of(i * 72, 8), 64), :].astype(BF16)

    def send_y(k, _):
        j = peer(k)
        pack(j)
        remote(ysend.at[j], yrecv.at[me], y_ssem, y_rsem, j).start()
        return 0

    lax.fori_loop(1, N, send_y, 0)
    own = ystg[pl.ds(pl.multiple_of(me * 72, 8), 64), :]
    yrecv[me] = jnp.zeros((64, HD), BF16)

    leg2_wait(2)
    par = parents[me]
    length = lens[par]
    source = table[length // 16, par]
    half = source % BLK // 3 * 2
    off = length % 16
    kept_all = p2y[pl.ds(half, 2)].astype(F32)
    stg[0 : 32 * 8, :] = kept_all.reshape(32 * 8, HD)
    slot = fresh[me] % BLK
    newkv = newkv_ref[...].astype(F32)
    for t in range(16):
        rows = slice(t * TOKROWS, (t + 1) * TOKROWS)
        where_t = jnp.full((TOKROWS, HD), t, jnp.int32)
        token = jnp.where(where_t < off, stg[rows, :], jnp.where(where_t == off, newkv, 0.0))
        for b in range(2):
            here = jnp.full((TOKROWS, HD), OLD + b, jnp.int32) == slot
            at_t = (b, t // 8, t // 2 % 4, slice(t % 2 * 2, t % 2 * 2 + 2))
            old = poolz[at_t].astype(F32).reshape(TOKROWS, HD)
            blk[at_t] = jnp.where(here, token, old).astype(BF16).reshape(2, 8, HD)
    new_copy = pltpu.make_async_copy(blk, newpool_ref.at[6:8], out_sem.at[2])
    new_copy.start()

    await_bytes(yrecv.at[0:63], y_rsem)

    def add(s, total):
        for k in range(4):
            total = total + yrecv[s * 4 + k].astype(F32)
        return total

    out_ref[...] = lax.fori_loop(0, N // 4, add, own)

    for phase in range(3):
        for p in range(3):
            await_bytes(q_region(phase, p), q_ssem.at[phase * 3 + p])
        await_bytes((rx, rz, ry)[phase].at[0:3], p_ssem.at[phase])
        await_bytes((p2x, p2z, p2y)[phase].at[0:3], p_ssem.at[3 + phase])
    for half in range(2):
        await_bytes(orecv.at[0:63, half * 2 : half * 2 + 2], o_ssem.at[half])
    await_bytes(srecv.at[0:63], s_ssem)
    await_bytes(ysend.at[0:63], y_ssem)
    new_copy.wait()
    for copy in keep_copies:
        copy.wait()


def local(
    queries, new_kv, prefix_kv, pool, out_weight, parents, tail_table, fresh_slots, tail_lengths
):
    def rows_of(a):
        lead = a.shape[:-2]
        a = a.reshape(lead + (2, KVH, HD))
        k = len(lead)
        return a.transpose(tuple(range(k)) + (k + 1, k, k + 2))

    kv = rows_of(prefix_kv).reshape(REQS, PRE * TOKROWS, HD)
    pool_rows = rows_of(pool).reshape(BLK, 2, 4, 4, 8, HD)
    new_rows = rows_of(new_kv).reshape(TOKROWS, HD)
    smem = pl.BlockSpec(memory_space=pltpu.SMEM)
    vmem = pl.BlockSpec(memory_space=pltpu.VMEM)
    hbm = pl.BlockSpec(memory_space=pl.ANY)
    dma = pltpu.SemaphoreType.DMA
    out, new_pool = pl.pallas_call(
        kernel,
        out_shape=(
            jax.ShapeDtypeStruct((64, HD), F32),
            jax.ShapeDtypeStruct((BLK, 2, 4, 4, 8, HD), BF16),
        ),
        in_specs=[smem] * 4 + [vmem, vmem, hbm, hbm, hbm],
        out_specs=(vmem, hbm),
        scratch_shapes=[
            pltpu.VMEM((CHUNKS, CHUNK * TOKROWS, HD), BF16),
            pltpu.VMEM((CHUNK * TOKROWS, HD), F32),
            pltpu.VMEM((REQS, KVH, 2, PRE, HD), BF16),
            pltpu.VMEM((KVH, 2, CHUNK, HD), BF16),
            pltpu.VMEM((2, 3, 2, 4, 4, 8, HD), BF16),
            pltpu.VMEM((2, 2, 4, 4, 8, HD), BF16),
            pltpu.VMEM((BEAMS * HQ, HD), F32),
            pltpu.VMEM((4, 4, 4, KVH, GROUPS, HD), BF16),
            pltpu.VMEM((REQS, KVH, 128, HD), BF16),
            pltpu.VMEM((N, 128), F32),
            pltpu.VMEM((REQS, HQ, BEAMS, HD), BF16),
            pltpu.VMEM((N, REQS, BEAMS, HD), BF16),
            pltpu.VMEM((HQ, 128), F32),
            pltpu.VMEM((128, 128), F32),
            pltpu.VMEM((HD, 8192), BF16),
            pltpu.VMEM((N * 72, HD), F32),
            pltpu.VMEM((N, 64, HD), BF16),
            pltpu.VMEM((N, 64, HD), BF16),
            pltpu.VMEM((4, 2, 3, 2, 4, 8, HD), BF16),
            pltpu.VMEM((4, 4, 2, 3, 2, 8, HD), BF16),
            pltpu.VMEM((4, 4, 4, 3, 8, HD), BF16),
            pltpu.VMEM((4, 4, 4, 8, HD), BF16),
            pltpu.VMEM((4, 4, 4, 8, HD), BF16),
            pltpu.VMEM((4, 4, 4, 8, HD), BF16),
            pltpu.VMEM((4, 4, 4, 8, HD), BF16),
            pltpu.VMEM((2, 2, 4, 4, 8, HD), BF16),
            dma((CHUNKS,)), dma((4,)), dma((3,)),
            dma((9,)), dma((9,)), dma((2,)), dma((2,)), dma, dma,
            dma, dma, dma((6,)), dma((6,)),
        ],
        compiler_params=pltpu.CompilerParams(
            collective_id=0, has_side_effects=True, vmem_limit_bytes=56 << 20
        ),
        name="beam_decode",
    )(
        parents, tail_table.T, fresh_slots, tail_lengths,
        queries, new_rows, kv, pool_rows, out_weight,
    )
    new_pool = new_pool.reshape(BLK, 16, KVH, 2, HD).transpose(0, 1, 3, 2, 4)
    return out.reshape(1, 8192), new_pool.reshape(BLK, 16, 2, KVH * HD)


def solution(mesh):
    in_specs = (
        P(("req", "ctx"), None),
        P(("req", "ctx"), None, None),
        P("req", "ctx", None, None),
        P(("req", "ctx"), None, None, None),
        P("ctx", None),
        P("req"),
        P("req", None),
        P("req"),
        P("req"),
    )
    out_specs = (P(("req", "ctx"), None), P(("req", "ctx"), None, None, None))
    return jax.shard_map(local, mesh=mesh, in_specs=in_specs, out_specs=out_specs, check_vma=False)
```

```python
import functools
import math

import jax
import jax.numpy as jnp
from jax import lax
from jax.experimental import pallas as pl
from jax.experimental.pallas import tpu as pltpu
from jax.sharding import PartitionSpec as P

KVH = 8
HD = 128
GROUPS = 8
HQ = 64
N = 64
REQS = 4
BEAMS = 16
PRE = 1024
CHUNK = 128
PER_REQ = PRE // CHUNK
CHUNKS = REQS * PER_REQ
TOKROWS = 16
BLK = 8
OLD = 6
NEG = -1e30
SCALE = HD ** (-0.5) * math.log2(math.e)
MESH = pl.DeviceIdType.MESH
F32 = jnp.float32
BF16 = jnp.bfloat16
PARTS = ((0, 3, "xzy"), (3, 6, "zyx"), (6, 8, "yxz"))


def dot_nt(a, b):
    return lax.dot_general(a, b, (((1,), (1,)), ((), ())), preferred_element_type=F32)


def dot_nn(a, b):
    return jnp.dot(a, b, preferred_element_type=F32)


def kernel(
    parents, table, fresh, lens, q_ref, newkv_ref, kv_hbm, pool_hbm, w_hbm,
    out_ref, newpool_ref,
    raw, stg, kd, kt, poolv, poolz, qstg, qbuf, qd, bias, osend, orecv, stat, srecv,
    wv, ystg, ysend, yrecv, rx, rz, ry, p2send, p2x, p2z, p2y, blk,
    kv_sem, misc_sem, out_sem, q_ssem, q_rsem, o_ssem, o_rsem, s_ssem, s_rsem,
    y_ssem, y_rsem, p_ssem, p_rsem,
):
    core = lax.axis_index("req")
    me = lax.axis_index("ctx")
    y, z, x = me // 16, me // 4 % 4, me % 4

    def at(dy, dz, dx):
        return ((y + dy) % 4 * 4 + (z + dz) % 4) * 4 + (x + dx) % 4

    def peer(k):
        return at(k // 16, k // 4 % 4, k % 4)

    def remote(src, dst, ssem, rsem, dev):
        return pltpu.make_async_remote_copy(
            src_ref=src, dst_ref=dst, send_sem=ssem, recv_sem=rsem,
            device_id=(core, dev), device_id_type=MESH,
        )

    def await_bytes(ref, sem):
        pltpu.make_async_copy(ref, ref, sem).wait()

    def kv_copy(c):
        return pltpu.make_async_copy(
            kv_hbm.at[c // PER_REQ, pl.ds(c % PER_REQ * (CHUNK * TOKROWS), CHUNK * TOKROWS)],
            raw.at[c], kv_sem.at[c],
        )

    barrier = pltpu.get_barrier_semaphore()
    for d in range(1, 4):
        for dev in (at(d, 0, 0), at(0, d, 0), at(0, 0, d)):
            pl.semaphore_signal(barrier, inc=1, device_id=(core, dev), device_id_type=MESH)

    pool_copies = [
        pltpu.make_async_copy(pool_hbm.at[0:3], poolv.at[0], misc_sem.at[0]),
        pltpu.make_async_copy(pool_hbm.at[3:6], poolv.at[1], misc_sem.at[1]),
        pltpu.make_async_copy(pool_hbm.at[6:8], poolz, misc_sem.at[2]),
    ]
    w_copy = pltpu.make_async_copy(w_hbm, wv, misc_sem.at[3])
    for copy in pool_copies:
        copy.start()

    def start_kv(c, _):
        kv_copy(c).start()
        return 0

    lax.fori_loop(0, CHUNKS, start_kv, 0)
    w_copy.start()

    for h in range(HQ):
        qstg[h : h + 1, :] = q_ref[:, h * HD : (h + 1) * HD].astype(F32)
    qbuf[y, z, x] = qstg[0:HQ, :].astype(BF16).reshape(KVH, GROUPS, HD)

    def q_copies(phase):
        made = []
        for p, (g0, g1, order) in enumerate(PARTS):
            axis = order[phase]
            seen = order[:phase]
            index = (
                slice(None) if "y" in seen else y,
                slice(None) if "z" in seen else z,
                slice(None) if "x" in seen else x,
                slice(g0, g1),
            )
            for d in range(1, 4):
                dev = at(d * (axis == "y"), d * (axis == "z"), d * (axis == "x"))
                made.append(remote(
                    qbuf.at[index], qbuf.at[index],
                    q_ssem.at[phase * 3 + p], q_rsem.at[phase * 3 + p], dev,
                ))
        return made

    def q_region(phase, p):
        g0, g1, _ = PARTS[p]
        rows = (
            (0, slice(0, 1), slice(0, 3)),
            (0, slice(0, 3), slice(None)),
            (slice(0, 3), slice(None), slice(None)),
        )[phase]
        return qbuf.at[rows + (slice(g0, g1),)]

    def q_send(phase):
        for copy in q_copies(phase):
            copy.start()

    def q_wait(phase):
        for p in range(3):
            await_bytes(q_region(phase, p), q_rsem.at[phase * 3 + p])

    for copy in pool_copies:
        copy.wait()
    keep_copies = [
        pltpu.make_async_copy(poolv.at[0], newpool_ref.at[0:3], out_sem.at[0]),
        pltpu.make_async_copy(poolv.at[1], newpool_ref.at[3:6], out_sem.at[1]),
    ]
    for copy in keep_copies:
        copy.start()

    def spread(dst, base):
        for j in range(TOKROWS):
            dst[j // 2, j % 2, pl.ds(base, CHUNK), :] = stg[
                pl.ds(j, CHUNK, stride=TOKROWS), :
            ].astype(BF16)

    stg[0 : OLD * 256, :] = poolv[...].reshape(OLD * 256, HD).astype(F32)
    stg[OLD * 256 :, :] = poolz[...].reshape((BLK - OLD) * 256, HD).astype(F32)
    stg[OLD * 256 : OLD * 256 + TOKROWS, :] = newkv_ref[...].astype(F32)
    spread(kt, 0)

    def along(d):
        return (y + d) % 4, (z + d) % 4, (x + d) % 4

    def leg1(phase):
        for d in range(1, 4):
            y2_, z2_, x2_ = along(d)
            src, dst, dev = (
                (poolv.at[:, :, :, :, x2_], rx.at[x], at(0, 0, d)),
                (rx.at[:, :, :, :, z2_], rz.at[z], at(0, d, 0)),
                (rz.at[:, :, y2_ // 2, :, y2_ % 2], ry.at[y], at(d, 0, 0)),
            )[phase]
            remote(src, dst, p_ssem.at[phase], p_rsem.at[phase], dev).start()
        if phase == 0:
            rx[x] = poolv[:, :, :, :, x]
        elif phase == 1:
            rz[z] = rx[:, :, :, :, z]
        else:
            ry[y] = rz[:, :, y // 2, :, y % 2]

    def leg1_wait(phase):
        await_bytes((rx, rz, ry)[phase].at[0:3], p_rsem.at[phase])

    def leg2(phase):
        for d in range(1, 4):
            y2_, z2_, x2_ = along(d)
            src, dst, dev = (
                (p2send.at[:, :, x2_], p2x.at[x], at(0, 0, d)),
                (p2x.at[:, :, z2_], p2z.at[z], at(0, d, 0)),
                (p2z.at[:, :, y2_], p2y.at[y], at(d, 0, 0)),
            )[phase]
            remote(src, dst, p_ssem.at[3 + phase], p_rsem.at[3 + phase], dev).start()
        if phase == 0:
            p2x[x] = p2send[:, :, x]
        elif phase == 1:
            p2z[z] = p2x[:, :, z]
        else:
            p2y[y] = p2z[:, :, y]

    def leg2_wait(phase):
        await_bytes((p2x, p2z, p2y)[phase].at[0:3], p_rsem.at[3 + phase])

    def chunks(lo, hi):
        def body(c, _):
            kv_copy(c).wait()
            stg[...] = raw[c].astype(F32)
            spread(kd.at[c // PER_REQ], pl.multiple_of(c % PER_REQ * CHUNK, CHUNK))
            return 0

        lax.fori_loop(lo, hi, body, 0)

    chunks(0, 4)
    pl.semaphore_wait(barrier, 9)
    q_send(0)
    leg1(0)

    lane = lax.broadcasted_iota(jnp.int32, (1, 128), 1)

    def mask_row(i, _):
        par = parents[i]
        length = lens[par]
        live = (lane == OLD * 16) & (jnp.full((1, 128), i, jnp.int32) == me)
        for j in range(4):
            block = table[j, par] - me * BLK
            live = live | ((lane // 16 == block) & (lane % 16 < length - 16 * j))
        bias[pl.ds(i, 1), :] = jnp.where(live, 0.0, NEG)
        return 0

    lax.fori_loop(0, N, mask_row, 0, unroll=8)

    chunks(4, 10)
    q_wait(0)
    q_send(1)
    chunks(10, 20)
    q_wait(1)
    q_send(2)
    leg1_wait(0)
    leg1(1)
    chunks(20, 32)
    q_wait(2)
    leg1_wait(1)
    leg1(2)

    first = me // 32 * 3

    def pick(i, _):
        par = parents[i]
        source = table[lens[par] // 16, par]
        held = jnp.clip(source % BLK - first, 0, 2)
        home = source // BLK
        p2send[i // 16, i // 4 % 4, i % 4] = ry[home // 16, home // 4 % 4, home % 4, held]
        return 0

    stat[...] = jnp.zeros_like(stat)
    sub16 = lax.broadcasted_iota(jnp.int32, (BEAMS, 128), 0)
    lane16 = lax.broadcasted_iota(jnp.int32, (BEAMS, 128), 1)

    def turn(r, _):
        for i in range(BEAMS):
            qstg[i * 72 : i * 72 + HQ, :] = qbuf[r, i // 4, i % 4].reshape(HQ, HD).astype(F32)
        for h in range(HQ):
            qd[r, h // GROUPS, h % GROUPS * BEAMS : (h % GROUPS + 1) * BEAMS, :] = qstg[
                pl.ds(h, BEAMS, stride=72), :
            ].astype(BF16)
        return 0

    lax.fori_loop(0, REQS, turn, 0)
    own_group = me // GROUPS

    def group_of(t):
        return (own_group + t) % KVH

    def attend(r, g):
        bias_r = bias[pl.ds(pl.multiple_of(r * BEAMS, BEAMS), BEAMS), :]
        bias_q = jnp.broadcast_to(bias_r[None], (GROUPS, BEAMS, 128)).reshape(128, 128)
        m_spot = lane16 == sub16 + r * BEAMS
        l_spot = lane16 == sub16 + r * BEAMS + 64
        q = qd[r, g]
        s = dot_nt(q, kd[r, g, 0])
        st = dot_nt(q, kt[g, 0]) + bias_q
        top = jnp.maximum(s.max(-1, keepdims=True), st.max(-1, keepdims=True))
        e = jnp.exp2((s - top) * SCALE)
        et = jnp.exp2((st - top) * SCALE)
        total = e.sum(-1, keepdims=True) + et.sum(-1, keepdims=True)
        o = dot_nn(e.astype(BF16), kd[r, g, 1]) + dot_nn(et.astype(BF16), kt[g, 1])
        osend[r, pl.ds(g * GROUPS, GROUPS)] = o.astype(BF16).reshape(GROUPS, BEAMS, HD)
        top3 = jnp.broadcast_to(top, (128, 128)).reshape(GROUPS, BEAMS, 128)
        total3 = jnp.broadcast_to(total, (128, 128)).reshape(GROUPS, BEAMS, 128)
        both = jnp.where(m_spot[None], top3, jnp.where(l_spot[None], total3, 0.0))
        rows = pl.ds(pl.multiple_of(g * GROUPS, GROUPS), GROUPS)
        stat[rows, :] = stat[rows, :] + both.sum(1)

    def send(half, g):
        pair = pl.ds(half * 2, 2)

        def to(j, _):
            dev = g * GROUPS + (me + j) % GROUPS
            remote(
                osend.at[pair, dev], orecv.at[me, pair], o_ssem.at[half], o_rsem.at[half], dev
            ).start()

            @pl.when(half == 1)
            def _():
                remote(stat.at[pl.ds(dev, 1)], srecv.at[pl.ds(me, 1)], s_ssem, s_rsem, dev).start()

            return 0

        lax.fori_loop(jnp.where(g == own_group, 1, 0), GROUPS, to, 0)

    def step(u, _):
        @pl.when(u == 6)
        def _():
            leg1_wait(2)
            lax.fori_loop(0, N, pick, 0, unroll=8)
            leg2(0)

        @pl.when(u == 11)
        def _():
            leg2_wait(0)
            leg2(1)

        half = u // KVH
        g = group_of(u)
        attend(half * 2, g)
        attend(half * 2 + 1, g)
        send(half, g)
        return 0

    lax.fori_loop(0, 2 * KVH, step, 0)
    leg2_wait(1)
    leg2(2)
    orecv[me] = osend[:, me]
    srecv[pl.ds(me, 1), :] = stat[pl.ds(me, 1), :]

    await_bytes(srecv.at[0:63], s_rsem)
    turned = srecv[...].T
    valid = lax.broadcasted_iota(jnp.int32, (64, 128), 1) < N
    tops = jnp.where(valid, turned[0:64], -3e38)
    sums = jnp.where(valid, turned[64:128], 0.0)
    top = tops.max(-1, keepdims=True)
    share = jnp.exp2((tops - top) * SCALE)
    share = share / (share * sums).sum(-1, keepdims=True)
    for half in range(2):
        await_bytes(orecv.at[0:63, half * 2 : half * 2 + 2], o_rsem.at[half])

    def merge(s, carry):
        acc, turning = carry
        for k in range(4):
            acc = acc + turning[:, k : k + 1] * orecv[s * 4 + k].reshape(64, HD).astype(F32)
        return acc, pltpu.roll(turning, 124, 1)

    acc, _ = lax.fori_loop(0, N // 4, merge, (jnp.zeros((64, HD), F32), share))
    attended = acc.astype(BF16)

    w_copy.wait()

    def project(c, _):
        part = dot_nn(attended, wv[:, pl.ds(pl.multiple_of(c * 512, 512), 512)])
        for j in range(4):
            ystg[pl.ds(c * 4 + j, N, stride=72), :] = part[:, j * HD : (j + 1) * HD]
        return 0

    lax.fori_loop(0, 16, project, 0, unroll=4)

    def pack(i):
        ysend[i] = ystg[pl.ds(pl.multiple_of(i * 72, 8), 64), :].astype(BF16)

    def send_y(k, _):
        j = peer(k)
        pack(j)
        remote(ysend.at[j], yrecv.at[me], y_ssem, y_rsem, j).start()
        return 0

    lax.fori_loop(1, N, send_y, 0, unroll=3)
    own = ystg[pl.ds(pl.multiple_of(me * 72, 8), 64), :]
    yrecv[me] = jnp.zeros((64, HD), BF16)

    leg2_wait(2)
    par = parents[me]
    length = lens[par]
    source = table[length // 16, par]
    half = source % BLK // 3 * 2
    off = length % 16
    kept_all = p2y[pl.ds(half, 2)].astype(F32)
    stg[0 : 32 * 8, :] = kept_all.reshape(32 * 8, HD)
    slot = fresh[me] % BLK
    newkv = newkv_ref[...].astype(F32)
    for t in range(16):
        rows = slice(t * TOKROWS, (t + 1) * TOKROWS)
        where_t = jnp.full((TOKROWS, HD), t, jnp.int32)
        token = jnp.where(where_t < off, stg[rows, :], jnp.where(where_t == off, newkv, 0.0))
        for b in range(2):
            here = jnp.full((TOKROWS, HD), OLD + b, jnp.int32) == slot
            at_t = (b, t // 8, t // 2 % 4, slice(t % 2 * 2, t % 2 * 2 + 2))
            old = poolz[at_t].astype(F32).reshape(TOKROWS, HD)
            blk[at_t] = jnp.where(here, token, old).astype(BF16).reshape(2, 8, HD)
    new_copy = pltpu.make_async_copy(blk, newpool_ref.at[6:8], out_sem.at[2])
    new_copy.start()

    await_bytes(yrecv.at[0:63], y_rsem)

    def add(s, total):
        for k in range(4):
            total = total + yrecv[s * 4 + k].astype(F32)
        return total

    out_ref[...] = lax.fori_loop(0, N // 4, add, own)

    for phase in range(3):
        for p in range(3):
            await_bytes(q_region(phase, p), q_ssem.at[phase * 3 + p])
        await_bytes((rx, rz, ry)[phase].at[0:3], p_ssem.at[phase])
        await_bytes((p2x, p2z, p2y)[phase].at[0:3], p_ssem.at[3 + phase])
    for half in range(2):
        await_bytes(orecv.at[0:63, half * 2 : half * 2 + 2], o_ssem.at[half])
    await_bytes(srecv.at[0:63], s_ssem)
    await_bytes(ysend.at[0:63], y_ssem)
    new_copy.wait()
    for copy in keep_copies:
        copy.wait()


def local(
    queries, new_kv, prefix_kv, pool, out_weight, parents, tail_table, fresh_slots, tail_lengths
):
    def rows_of(a):
        lead = a.shape[:-2]
        a = a.reshape(lead + (2, KVH, HD))
        k = len(lead)
        return a.transpose(tuple(range(k)) + (k + 1, k, k + 2))

    kv = rows_of(prefix_kv).reshape(REQS, PRE * TOKROWS, HD)
    pool_rows = rows_of(pool).reshape(BLK, 2, 4, 4, 8, HD)
    new_rows = rows_of(new_kv).reshape(TOKROWS, HD)
    smem = pl.BlockSpec(memory_space=pltpu.SMEM)
    vmem = pl.BlockSpec(memory_space=pltpu.VMEM)
    hbm = pl.BlockSpec(memory_space=pl.ANY)
    dma = pltpu.SemaphoreType.DMA
    out, new_pool = pl.pallas_call(
        kernel,
        out_shape=(
            jax.ShapeDtypeStruct((64, HD), F32),
            jax.ShapeDtypeStruct((BLK, 2, 4, 4, 8, HD), BF16),
        ),
        in_specs=[smem] * 4 + [vmem, vmem, hbm, hbm, hbm],
        out_specs=(vmem, hbm),
        scratch_shapes=[
            pltpu.VMEM((CHUNKS, CHUNK * TOKROWS, HD), BF16),
            pltpu.VMEM((CHUNK * TOKROWS, HD), F32),
            pltpu.VMEM((REQS, KVH, 2, PRE, HD), BF16),
            pltpu.VMEM((KVH, 2, CHUNK, HD), BF16),
            pltpu.VMEM((2, 3, 2, 4, 4, 8, HD), BF16),
            pltpu.VMEM((2, 2, 4, 4, 8, HD), BF16),
            pltpu.VMEM((BEAMS * 72, HD), F32),
            pltpu.VMEM((4, 4, 4, KVH, GROUPS, HD), BF16),
            pltpu.VMEM((REQS, KVH, 128, HD), BF16),
            pltpu.VMEM((N, 128), F32),
            pltpu.VMEM((REQS, HQ, BEAMS, HD), BF16),
            pltpu.VMEM((N, REQS, BEAMS, HD), BF16),
            pltpu.VMEM((HQ, 128), F32),
            pltpu.VMEM((128, 128), F32),
            pltpu.VMEM((HD, 8192), BF16),
            pltpu.VMEM((N * 72, HD), F32),
            pltpu.VMEM((N, 64, HD), BF16),
            pltpu.VMEM((N, 64, HD), BF16),
            pltpu.VMEM((4, 2, 3, 2, 4, 8, HD), BF16),
            pltpu.VMEM((4, 4, 2, 3, 2, 8, HD), BF16),
            pltpu.VMEM((4, 4, 4, 3, 8, HD), BF16),
            pltpu.VMEM((4, 4, 4, 8, HD), BF16),
            pltpu.VMEM((4, 4, 4, 8, HD), BF16),
            pltpu.VMEM((4, 4, 4, 8, HD), BF16),
            pltpu.VMEM((4, 4, 4, 8, HD), BF16),
            pltpu.VMEM((2, 2, 4, 4, 8, HD), BF16),
            dma((CHUNKS,)), dma((4,)), dma((3,)),
            dma((9,)), dma((9,)), dma((2,)), dma((2,)), dma, dma,
            dma, dma, dma((6,)), dma((6,)),
        ],
        compiler_params=pltpu.CompilerParams(
            collective_id=0, has_side_effects=True, vmem_limit_bytes=56 << 20
        ),
        name="beam_decode",
    )(
        parents, tail_table.T, fresh_slots, tail_lengths,
        queries, new_rows, kv, pool_rows, out_weight,
    )
    new_pool = new_pool.reshape(BLK, 16, KVH, 2, HD).transpose(0, 1, 3, 2, 4)
    return out.reshape(1, 8192), new_pool.reshape(BLK, 16, 2, KVH * HD)


def solution(mesh):
    in_specs = (
        P(("req", "ctx"), None),
        P(("req", "ctx"), None, None),
        P("req", "ctx", None, None),
        P(("req", "ctx"), None, None, None),
        P("ctx", None),
        P("req"),
        P("req", None),
        P("req"),
        P("req"),
    )
    out_specs = (P(("req", "ctx"), None), P(("req", "ctx"), None, None, None))
    return jax.shard_map(local, mesh=mesh, in_specs=in_specs, out_specs=out_specs, check_vma=False)
```
